32 devices in a mesh: row: 4 (over x, core), col: 2 (over y), depth: 4 (over z).
Axes of the slice: x: 2, y: 2, z: 4, core: 2. Of those that a mesh axis runs over, the one named last changes fastest.
Arguments:
- tokens: bfloat16 [64, 6144], P(('col', 'depth'), 'row'), may hold values from -6 to 6
- first_weight: bfloat16 [6144, 24576], P('row', ('col', 'depth')), may hold values from -0.078125 to 0.078125
- first_tangent: bfloat16 [6144, 24576], P('row', ('col', 'depth')), may hold values from -0.078125 to 0.078125
- second_weight: bfloat16 [24576, 6144], P(('col', 'depth'), 'row'), may hold values from -0.0390625 to 0.0390625
- second_tangent: bfloat16 [24576, 6144], P(('col', 'depth'), 'row'), may hold values from -0.0390625 to 0.0390625
Outputs:
- grad_first: float32 [6144, 24576], P('row', ('col', 'depth'))
- grad_second: float32 [24576, 6144], P(('col', 'depth'), 'row')
The draws below stay inside these ranges and needn't reach their ends.
All inputs are finite; a program needn't handle non-finite values.
Results may differ from the reference program's by a relative error of at most 0.0047.
Values may be sent and summed in bfloat16 or wider, within the bound.
A program may use at most 192 MiB of HBM per device.

```python
import math
import jax
import jax.numpy as jnp
from jax import lax

D = 6144
FF = 24576
TOKENS = 64


def shard_levels(stream_key, extent, split, smallest, high):
    gain = 1.0
    for axis_at, blocks in split:
        steps = jax.random.uniform(jax.random.fold_in(jax.random.fold_in(stream_key, 6), axis_at), (blocks,), jnp.float32, smallest / len(split), high / len(split))
        gain = gain * jnp.repeat(jnp.exp(steps), extent[axis_at] // blocks).reshape((-1,) + (1,) * (len(extent) - 1 - axis_at))
    return gain


def centred(stream_key, shape, width, bound, split=(), held_as=jnp.bfloat16):
    array = width * jax.random.normal(stream_key, shape, jnp.float32)
    if split:
        array = array * shard_levels(stream_key, shape, split, -0.22, 0.18)
    return jnp.clip(array, -bound, bound).astype(held_as)


def setup_inputs(seed: int = 0) -> dict:
    seeds = jax.random.split(jax.random.key(seed), 6)
    return {
        "tokens": centred(seeds[0], (TOKENS, D), 1.0, 6.0, ((0, 8), (1, 4))),
        "first_weight": centred(seeds[1], (D, FF), D ** -0.5, 0.078125, ((0, 4), (1, 8))),
        "first_tangent": centred(seeds[2], (D, FF), D ** -0.5, 0.078125, ((0, 4), (1, 8))),
        "second_weight": centred(seeds[3], (FF, D), FF ** -0.5, 0.0390625, ((0, 8), (1, 4))),
        "second_tangent": centred(seeds[4], (FF, D), FF ** -0.5, 0.0390625, ((0, 8), (1, 4))),
    }


def reference(tokens, first_weight, first_tangent, second_weight, second_tangent):
    hidden = jnp.dot(tokens, first_weight, preferred_element_type=jnp.float32)
    hidden_tan = jnp.dot(tokens, first_tangent, preferred_element_type=jnp.float32)
    inner = 0.7978845608 * (hidden + 0.044715 * hidden * hidden * hidden)
    tval = jnp.tanh(inner)
    active = (0.5 * hidden * (1.0 + tval)).astype(jnp.bfloat16)
    slopes = 0.5 * (1.0 + tval) + 0.5 * hidden * (1.0 - tval * tval) * 0.7978845608 * (1.0 + 3.0 * 0.044715 * hidden * hidden)
    active_tan = (slopes * hidden_tan).astype(jnp.bfloat16)
    out_tan = (jnp.dot(active_tan, second_weight, preferred_element_type=jnp.float32) + jnp.dot(active, second_tangent, preferred_element_type=jnp.float32)).astype(jnp.bfloat16)
    backward = lax.dot_general(out_tan, second_weight, (((1,), (1,)), ((), ())), preferred_element_type=jnp.float32)
    back_hidden = (backward * slopes).astype(jnp.bfloat16)
    factor = 1.0 / math.sqrt(TOKENS)
    grad_second = lax.dot_general(active, out_tan, (((0,), (0,)), ((), ())), preferred_element_type=jnp.float32) * factor
    grad_first = lax.dot_general(tokens, back_hidden, (((0,), (0,)), ((), ())), preferred_element_type=jnp.float32) * factor
    return (grad_first, grad_second)
```

```python
import functools
import math

import jax
import jax.numpy as jnp
from jax import lax
from jax.experimental import pallas as pl
from jax.experimental.pallas import tpu as pltpu
from jax.sharding import PartitionSpec as P

CORES = 2
LAG_CHIP, LAG_SECOND = 3, 2
VMEM_MIB, GRADS_MIB, GROUPS, STEPS = 52, 30, 3, 12
LANES = 128
F32 = jnp.float32
BF16 = jnp.bfloat16


def pieces(extent, most):
    return max(n for n in range(1, most + 1) if extent % (n * LANES) == 0)


def gelu_parts(hidden, hidden_tan):
    inner = 0.7978845608 * (hidden + 0.044715 * hidden * hidden * hidden)
    tval = jnp.tanh(inner)
    active = 0.5 * hidden * (1.0 + tval)
    slopes = 0.5 * (1.0 + tval) + 0.5 * hidden * (1.0 - tval * tval) * 0.7978845608 * (
        1.0 + 3.0 * 0.044715 * hidden * hidden
    )
    return active, slopes * hidden_tan, slopes


def block_kernel(
    sizes,
    tok_ref, fw_ref, ft_ref, sw_ref, st_ref,
    tok_out, act_out, tan2d, cross_out, sum_out, slopes,
    w1, w2, tokg, tok2d, hbuf, precv, xsend, xrecv, acts,
    acc, rsend, rrecv, outg, bbuf, brecv,
    wsem, own_s, tok_s, tok_r,
    ps, pr, xs, xr, as_, ar, rs, rr, gs, gr, bps, bpr,
):
    chips, ncol, ndepth, nw, nf, no = sizes
    group = ncol * ndepth
    tl, dl = tok_ref.shape
    total = group * tl
    half = total // CORES
    ww = w1.shape[-1]
    fl = nw * ww
    cw, dn = fl // nf, dl // no

    row = lax.axis_index("row")
    core = lax.rem(row, CORES)
    chip = lax.div(row, CORES)
    mate = {"row": chip * CORES + (1 - core)}
    across = [{"row": lax.rem(chip + o, chips) * CORES + core} for o in range(1, chips)]
    me = lax.axis_index("col") * ndepth + lax.axis_index("depth")
    ranks = [lax.rem(me + o, group) for o in range(1, group)]
    peers = [{"col": lax.div(r, ndepth), "depth": lax.rem(r, ndepth)} for r in ranks]
    mine = pl.ds(pl.multiple_of(core * half, half), half)
    other = pl.ds(pl.multiple_of((1 - core) * half, half), half)

    barrier = pltpu.get_barrier_semaphore()
    entry = [mate] + across + peers
    for device in entry:
        pl.semaphore_signal(
            barrier, inc=1, device_id=device, device_id_type=pl.DeviceIdType.MESH
        )

    own = pltpu.make_async_copy(tok_ref, tokg.at[me], own_s)
    own.start()
    loads = {}
    for i, ref in enumerate((fw_ref, ft_ref)):
        for k in range(nw):
            loads[i, k] = pltpu.make_async_copy(
                ref.at[:, pl.ds(k * ww, ww)], w1.at[i, k], wsem.at[i, k]
            )
    for i, ref in enumerate((sw_ref, st_ref)):
        for k in range(nw):
            loads[2 + i, k] = pltpu.make_async_copy(
                ref.at[pl.ds(k * ww, ww), :], w2.at[i, k], wsem.at[2 + i, k]
            )
    for pair in (0, 2):
        for k in range(nw):
            loads[pair, k].start()
            loads[pair + 1, k].start()
    loaded = set()

    def load(i, k):
        if (i, k) not in loaded:
            loaded.add((i, k))
            loads[i, k].wait()

    sent = []

    def send(src, dst, ssem, rsem, device):
        copy = pltpu.make_async_remote_copy(
            src_ref=src, dst_ref=dst, send_sem=ssem, recv_sem=rsem,
            device_id=device, device_id_type=pl.DeviceIdType.MESH,
        )
        copy.start()
        sent.append(copy)
        return copy

    own.wait()
    pl.semaphore_wait(barrier, len(entry))

    arrivals = [
        send(tokg.at[me], tokg.at[me], tok_s.at[o], tok_r.at[o], device)
        for o, device in enumerate(peers)
    ]
    for copy in arrivals:
        copy.wait_recv()
    tok2d[...] = tokg[...].astype(F32).reshape(total, dl).astype(BF16)

    tok_out[pl.ds(0, half), :] = tok2d[mine, :]
    tok_out[pl.ds(half, half), :] = tok2d[other, :]

    cols = [pl.ds(k * cw, cw) for k in range(nf)]
    to_mate, to_chips, halves = {}, {}, {}
    per = nf // nw

    for i in range(2):
        for k in range(nw):
            load(i, k)

    def first(k):
        for i in range(2):
            weight = w1[i, k // per, :, pl.ds((k % per) * cw, cw)]
            hbuf[i, :, cols[k]] = jnp.dot(tok2d[...], weight, preferred_element_type=F32)
        to_mate[k] = send(hbuf.at[:, other, cols[k]], precv.at[k], ps.at[k], pr.at[k], mate)

    def chip_sum(k):
        to_mate[k].wait_recv()
        for i in range(2):
            both = hbuf[i, mine, cols[k]] + precv[k, i]
            hbuf[i, mine, cols[k]] = both
            xsend[k, i] = both.astype(BF16)
        to_chips[k] = [
            send(xsend.at[k], xrecv.at[o, k], xs.at[o, k], xr.at[o, k], device)
            for o, device in enumerate(across)
        ]

    def activate(k):
        hidden, hidden_tan = hbuf[0, mine, cols[k]], hbuf[1, mine, cols[k]]
        for o, copy in enumerate(to_chips[k]):
            copy.wait_recv()
            hidden = hidden + xrecv[o, k, 0].astype(F32)
            hidden_tan = hidden_tan + xrecv[o, k, 1].astype(F32)
        active, active_tan, slope = gelu_parts(hidden, hidden_tan)
        acts[0, mine, cols[k]] = active_tan.astype(BF16)
        acts[1, mine, cols[k]] = active.astype(BF16)
        slopes[:, cols[k]] = slope
        part = acts.at[:, mine, cols[k]]
        halves[k] = send(part, part, as_.at[k], ar.at[k], mate)

    scatter, gather = {}, {}

    def second(k, begin, last):
        for j in range(begin, k + 1):
            halves[j].wait_recv()
        w, base = begin // per, (begin % per) * cw
        span, here = (k + 1 - begin) * cw, pl.ds(begin * cw, (k + 1 - begin) * cw)
        for i in range(2):
            load(2 + i, w)
        for n in range(no):
            part = pl.ds(n * dn, dn)
            term = None
            for i in range(2):
                product = jnp.dot(
                    acts[i, :, here], w2[i, w, pl.ds(base, span), part], preferred_element_type=F32
                )
                term = product if term is None else term + product
            if begin > 0:
                term += acc[n]
            acc[n] = term
            if last:
                rsend[n] = term.reshape(group, tl, dn).astype(BF16)
                scatter[n] = [
                    send(rsend.at[n, r], rrecv.at[n, o], rs.at[n, o], rr.at[n, o], device)
                    for o, (r, device) in enumerate(zip(ranks, peers))
                ]

    for t in range(nf + LAG_CHIP):
        if t < nf:
            first(t)
        if t >= LAG_CHIP:
            chip_sum(t - LAG_CHIP)
    begin = 0
    for t in range(nf + LAG_SECOND):
        if t < nf:
            activate(t)
        k = t - LAG_SECOND
        if k >= 0 and ((k + 1) % per == 0 or k // per == nw - 1):
            second(k, begin, k == nf - 1)
            begin = k + 1
    act_out[...] = acts[1]

    for n in range(no):
        value = acc[n, pl.ds(pl.multiple_of(me * tl, tl), tl), :]
        for o, copy in enumerate(scatter[n]):
            copy.wait_recv()
            value += rrecv[n, o].astype(F32)
        outg[n, me] = value.astype(BF16)
        gather[n] = [
            send(outg.at[n, me], outg.at[n, me], gs.at[n, o], gr.at[n, o], device)
            for o, device in enumerate(peers)
        ]

    to_mate = {}
    wide = nf // GROUPS if nf % GROUPS == 0 else 1

    def back_chip_sum(g):
        to_mate[g].wait_recv()
        span = pl.ds(g * wide * cw, wide * cw)
        both = bbuf[mine, span] + brecv[g]
        sum_out[:, span] = both
        cross_out[:, span] = both.astype(BF16)

    for n in range(no):
        for copy in gather[n]:
            copy.wait_recv()
        part = pl.ds(n * dn, dn)
        tan2d[:, part] = outg[n].astype(F32).reshape(total, dn).astype(BF16)
        for k in range(nf):
            term = lax.dot_general(
                tan2d[:, part], w2[0, k // per, pl.ds((k % per) * cw, cw), part],
                (((1,), (1,)), ((), ())), preferred_element_type=F32,
            )
            if n > 0:
                term += bbuf[:, cols[k]]
            bbuf[:, cols[k]] = term
            if n == no - 1 and (k + 1) % wide == 0:
                g = k // wide
                span = pl.ds(g * wide * cw, wide * cw)
                to_mate[g] = send(bbuf.at[other, span], brecv.at[g], bps.at[g], bpr.at[g], mate)
    for g in range(nf // wide):
        back_chip_sum(g)
    for copy in sent:
        copy.wait_send()


def second_kernel(factor, act_ref, tan_ref, out_ref, buf, sem):
    n, step = buf.shape[:2]
    copies = []
    for j in range(n):
        part = pl.ds(j * step, step)
        buf[j] = factor * lax.dot_general(
            act_ref[:, part], tan_ref[...], (((0,), (0,)), ((), ())), preferred_element_type=F32
        )
        copy = pltpu.make_async_copy(buf.at[j], out_ref.at[part, :], sem.at[j])
        copy.start()
        copies.append(copy)
    for copy in copies:
        copy.wait()


def first_kernel(factor, tok_ref, own_ref, mate_ref, out_ref, both, buf, sem):
    n, step = buf.shape[:2]
    half = own_ref.shape[0]
    both[pl.ds(0, half), :] = own_ref[...]
    both[pl.ds(half, half), :] = mate_ref[...]
    copies = []
    for j in range(n):
        part = pl.ds(j * step, step)
        buf[j] = factor * lax.dot_general(
            tok_ref[:, part], both[...], (((0,), (0,)), ((), ())), preferred_element_type=F32
        )
        copy = pltpu.make_async_copy(buf.at[j], out_ref.at[part, :], sem.at[j])
        copy.start()
        copies.append(copy)
    for copy in copies:
        copy.wait()


def on_device(axes, tokens, first_weight, first_tangent, second_weight, second_tangent):
    tl, dl = tokens.shape
    fl = first_weight.shape[1]
    ncol, ndepth, chips = axes["col"], axes["depth"], axes["row"] // CORES
    group = ncol * ndepth
    total, half = group * tl, group * tl // CORES
    nw, no = pieces(fl, 6), pieces(dl, 3)
    nf = 2 * nw if (fl // nw) % (2 * LANES) == 0 else nw
    cw, ww, dn = fl // nf, fl // nw, dl // no
    far = max(chips - 1, 1)
    groups = GROUPS if nf % GROUPS == 0 else nf
    factor = 1.0 / math.sqrt(total)
    dma = pltpu.SemaphoreType.DMA
    hbm = pl.BlockSpec(memory_space=pl.ANY)
    vmem = pl.BlockSpec(memory_space=pltpu.VMEM)
    gathered, active, out_tan, cross, own_sum, slopes = pl.pallas_call(
        functools.partial(block_kernel, (chips, ncol, ndepth, nw, nf, no)),
        name="block",
        out_shape=(
            jax.ShapeDtypeStruct((total, dl), BF16),
            jax.ShapeDtypeStruct((total, fl), BF16),
            jax.ShapeDtypeStruct((total, dl), BF16),
            jax.ShapeDtypeStruct((half, fl), BF16),
            jax.ShapeDtypeStruct((half, fl), F32),
            jax.ShapeDtypeStruct((half, fl), F32),
        ),
        in_specs=[hbm] * 5,
        out_specs=(vmem,) * 6,
        scratch_shapes=[
            pltpu.VMEM((2, nw, dl, ww), BF16),
            pltpu.VMEM((2, nw, ww, dl), BF16),
            pltpu.VMEM((group, tl, dl), BF16),
            pltpu.VMEM((total, dl), BF16),
            pltpu.VMEM((2, total, fl), F32),
            pltpu.VMEM((nf, 2, half, cw), F32),
            pltpu.VMEM((nf, 2, half, cw), BF16),
            pltpu.VMEM((far, nf, 2, half, cw), BF16),
            pltpu.VMEM((2, total, fl), BF16),
            pltpu.VMEM((no, total, dn), F32),
            pltpu.VMEM((no, group, tl, dn), BF16),
            pltpu.VMEM((no, group - 1, tl, dn), BF16),
            pltpu.VMEM((no, group, tl, dn), BF16),
            pltpu.VMEM((total, fl), F32),
            pltpu.VMEM((groups, half, fl // groups), F32),
            dma((4, nw)),
            dma,
            dma((group - 1,)), dma((group - 1,)),
            dma((nf,)), dma((nf,)),
            dma((far, nf)), dma((far, nf)),
            dma((nf,)), dma((nf,)),
            dma((no, group - 1)), dma((no, group - 1)),
            dma((no, group - 1)), dma((no, group - 1)),
            dma((groups,)), dma((groups,)),
        ],
        compiler_params=pltpu.CompilerParams(
            collective_id=0, has_side_effects=True, vmem_limit_bytes=VMEM_MIB * 1024 * 1024
        ),
    )(tokens, first_weight, first_tangent, second_weight, second_tangent)

    rows = range(chips * CORES)
    value = own_sum
    arrived = [
        lax.ppermute(cross, "row", [(r, (r + o * CORES) % (chips * CORES)) for r in rows])
        for o in range(1, chips)
    ]
    ns, nd = pieces(fl, STEPS), pieces(dl, STEPS)
    cost = pl.CostEstimate(flops=2 * total * fl * dl, bytes_accessed=4 * fl * dl, transcendentals=0)
    params = pltpu.CompilerParams(vmem_limit_bytes=GRADS_MIB * 1024 * 1024)
    grad_second = pl.pallas_call(
        functools.partial(second_kernel, factor),
        name="second",
        out_shape=jax.ShapeDtypeStruct((fl, dl), F32),
        in_specs=[vmem] * 2,
        out_specs=hbm,
        scratch_shapes=[pltpu.VMEM((ns, fl // ns, dl), F32), dma((ns,))],
        cost_estimate=cost,
        compiler_params=params,
    )(active, out_tan)
    arrived, grad_second = lax.optimization_barrier((arrived, grad_second))
    for part in arrived:
        value = value + part.astype(F32)
    back = (value * slopes).astype(BF16)
    other = lax.ppermute(back, "row", [(r, r + 1 - 2 * (r % CORES)) for r in rows])
    grad_first = pl.pallas_call(
        functools.partial(first_kernel, factor),
        name="first",
        out_shape=jax.ShapeDtypeStruct((dl, fl), F32),
        in_specs=[vmem] * 3,
        out_specs=hbm,
        scratch_shapes=[
            pltpu.VMEM((total, fl), BF16), pltpu.VMEM((nd, dl // nd, fl), F32), dma((nd,))
        ],
        cost_estimate=cost,
        compiler_params=params,
    )(gathered, back, other)
    return grad_first, grad_second


def solution(mesh):
    return jax.shard_map(
        functools.partial(on_device, dict(mesh.shape)),
        mesh=mesh,
        in_specs=(
            P(("col", "depth"), "row"),
            P("row", ("col", "depth")),
            P("row", ("col", "depth")),
            P(("col", "depth"), "row"),
            P(("col", "depth"), "row"),
        ),
        out_specs=(P("row", ("col", "depth")), P(("col", "depth"), "row")),
        check_vma=False,
    )
```

```python
import functools
import math

import jax
import jax.numpy as jnp
from jax import lax
from jax.experimental import pallas as pl
from jax.experimental.pallas import tpu as pltpu
from jax.sharding import PartitionSpec as P

CORES = 2
LAG_CHIP, LAG_SECOND = 3, 2
VMEM_MIB, GRADS_MIB, GROUPS, STEPS = 52, 30, 3, 12
LANES = 128
F32 = jnp.float32
BF16 = jnp.bfloat16


def pieces(extent, most):
    return max(n for n in range(1, most + 1) if extent % (n * LANES) == 0)


def gelu_parts(hidden, hidden_tan):
    inner = 0.7978845608 * (hidden + 0.044715 * hidden * hidden * hidden)
    tval = jnp.tanh(inner)
    active = 0.5 * hidden * (1.0 + tval)
    slopes = 0.5 * (1.0 + tval) + 0.5 * hidden * (1.0 - tval * tval) * 0.7978845608 * (
        1.0 + 3.0 * 0.044715 * hidden * hidden
    )
    return active, slopes * hidden_tan, slopes


def block_kernel(
    sizes,
    tok_ref, fw_ref, ft_ref, sw_ref, st_ref,
    tok_out, act_out, tan2d, cross_out, sum_out, slopes,
    w1, w2, tokg, tok2d, hbuf, precv, xsend, xrecv, acts,
    acc, rsend, rrecv, outg, bbuf, brecv,
    wsem, own_s, tok_s, tok_r,
    ps, pr, xs, xr, as_, ar, rs, rr, gs, gr, bps, bpr,
):
    chips, ncol, ndepth, nw, nf, no = sizes
    group = ncol * ndepth
    tl, dl = tok_ref.shape
    total = group * tl
    half = total // CORES
    ww = w1.shape[-1]
    fl = nw * ww
    cw, dn = fl // nf, dl // no

    row = lax.axis_index("row")
    core = lax.rem(row, CORES)
    chip = lax.div(row, CORES)
    mate = {"row": chip * CORES + (1 - core)}
    across = [{"row": lax.rem(chip + o, chips) * CORES + core} for o in range(1, chips)]
    me = lax.axis_index("col") * ndepth + lax.axis_index("depth")
    ranks = [lax.rem(me + o, group) for o in range(1, group)]
    peers = [{"col": lax.div(r, ndepth), "depth": lax.rem(r, ndepth)} for r in ranks]
    mine = pl.ds(pl.multiple_of(core * half, half), half)
    other = pl.ds(pl.multiple_of((1 - core) * half, half), half)

    barrier = pltpu.get_barrier_semaphore()
    entry = [mate] + across + peers
    for device in entry:
        pl.semaphore_signal(
            barrier, inc=1, device_id=device, device_id_type=pl.DeviceIdType.MESH
        )

    own = pltpu.make_async_copy(tok_ref, tokg.at[me], own_s)
    own.start()
    loads = {}
    for i, ref in enumerate((fw_ref, ft_ref)):
        for k in range(nw):
            loads[i, k] = pltpu.make_async_copy(
                ref.at[:, pl.ds(k * ww, ww)], w1.at[i, k], wsem.at[0]
            )
    for i, ref in enumerate((sw_ref, st_ref)):
        for k in range(nw):
            loads[2 + i, k] = pltpu.make_async_copy(
                ref.at[pl.ds(k * ww, ww), :], w2.at[i, k], wsem.at[1]
            )
    for pair in (0, 2):
        for k in range(nw):
            loads[pair, k].start()
            loads[pair + 1, k].start()
    def send(src, dst, ssem, rsem, device):
        copy = pltpu.make_async_remote_copy(
            src_ref=src, dst_ref=dst, send_sem=ssem, recv_sem=rsem,
            device_id=device, device_id_type=pl.DeviceIdType.MESH,
        )
        copy.start()
        return copy

    def all_of(ref, sem):
        pltpu.make_async_copy(ref, ref, sem).wait()

    own.wait()
    pl.semaphore_wait(barrier, len(entry))

    for device in peers:
        send(tokg.at[me], tokg.at[me], tok_s, tok_r, device)
    all_of(tokg.at[pl.ds(0, group - 1)], tok_r)
    tok2d[...] = tokg[...].astype(F32).reshape(total, dl).astype(BF16)

    tok_out[pl.ds(0, half), :] = tok2d[mine, :]
    tok_out[pl.ds(half, half), :] = tok2d[other, :]

    cols = [pl.ds(k * cw, cw) for k in range(nf)]
    to_mate, to_chips, halves = {}, {}, {}
    per = nf // nw

    all_of(w1, wsem.at[0])

    def first(k):
        for i in range(2):
            weight = w1[i, k // per, :, pl.ds((k % per) * cw, cw)]
            hbuf[i, :, cols[k]] = jnp.dot(tok2d[...], weight, preferred_element_type=F32)
        to_mate[k] = send(hbuf.at[:, other, cols[k]], precv.at[k], ps, pr.at[k], mate)

    def chip_sum(k):
        to_mate[k].wait_recv()
        for i in range(2):
            both = hbuf[i, mine, cols[k]] + precv[k, i]
            hbuf[i, mine, cols[k]] = both
            xsend[k, i] = both.astype(BF16)
        to_chips[k] = [
            send(xsend.at[k], xrecv.at[o, k], xs, xr.at[o, k], device)
            for o, device in enumerate(across)
        ]

    def activate(k):
        hidden, hidden_tan = hbuf[0, mine, cols[k]], hbuf[1, mine, cols[k]]
        for o, copy in enumerate(to_chips[k]):
            copy.wait_recv()
            hidden = hidden + xrecv[o, k, 0].astype(F32)
            hidden_tan = hidden_tan + xrecv[o, k, 1].astype(F32)
        active, active_tan, slope = gelu_parts(hidden, hidden_tan)
        acts[0, mine, cols[k]] = active_tan.astype(BF16)
        acts[1, mine, cols[k]] = active.astype(BF16)
        slopes[:, cols[k]] = slope
        part = acts.at[:, mine, cols[k]]
        halves[k] = send(part, part, as_, ar.at[k], mate)

    def second(k, begin, last):
        for j in range(begin, k + 1):
            halves[j].wait_recv()
        w, base = begin // per, (begin % per) * cw
        span, here = (k + 1 - begin) * cw, pl.ds(begin * cw, (k + 1 - begin) * cw)
        if begin == 0:
            all_of(w2, wsem.at[1])
        for n in range(no):
            part = pl.ds(n * dn, dn)
            term = None
            for i in range(2):
                product = jnp.dot(
                    acts[i, :, here], w2[i, w, pl.ds(base, span), part], preferred_element_type=F32
                )
                term = product if term is None else term + product
            if begin > 0:
                term += acc[n]
            acc[n] = term
            if last:
                rsend[n] = term.reshape(group, tl, dn).astype(BF16)
                for o, (r, device) in enumerate(zip(ranks, peers)):
                    send(rsend.at[n, r], rrecv.at[n, o], rs, rr.at[n], device)

    for t in range(nf + LAG_CHIP):
        if t < nf:
            first(t)
        if t >= LAG_CHIP:
            chip_sum(t - LAG_CHIP)
    begin = 0
    for t in range(nf + LAG_SECOND):
        if t < nf:
            activate(t)
        k = t - LAG_SECOND
        if k >= 0 and ((k + 1) % per == 0 or k // per == nw - 1):
            second(k, begin, k == nf - 1)
            begin = k + 1
    act_out[...] = acts[1]

    for n in range(no):
        value = acc[n, pl.ds(pl.multiple_of(me * tl, tl), tl), :]
        all_of(rrecv.at[n], rr.at[n])
        for o in range(group - 1):
            value += rrecv[n, o].astype(F32)
        outg[n, me] = value.astype(BF16)
        for device in peers:
            send(outg.at[n, me], outg.at[n, me], gs, gr.at[n], device)

    to_mate = {}
    wide = nf // GROUPS if nf % GROUPS == 0 else 1

    def back_chip_sum(g):
        to_mate[g].wait_recv()
        span = pl.ds(g * wide * cw, wide * cw)
        both = bbuf[mine, span] + brecv[g]
        sum_out[:, span] = both
        cross_out[:, span] = both.astype(BF16)

    for n in range(no):
        all_of(outg.at[n, pl.ds(0, group - 1)], gr.at[n])
        part = pl.ds(n * dn, dn)
        tan2d[:, part] = outg[n].astype(F32).reshape(total, dn).astype(BF16)
        for k in range(nf):
            term = lax.dot_general(
                tan2d[:, part], w2[0, k // per, pl.ds((k % per) * cw, cw), part],
                (((1,), (1,)), ((), ())), preferred_element_type=F32,
            )
            if n > 0:
                term += bbuf[:, cols[k]]
            bbuf[:, cols[k]] = term
            if n == no - 1 and (k + 1) % wide == 0:
                g = k // wide
                span = pl.ds(g * wide * cw, wide * cw)
                to_mate[g] = send(bbuf.at[other, span], brecv.at[g], bps, bpr.at[g], mate)
    for g in range(nf // wide):
        back_chip_sum(g)
    all_of(tokg.at[pl.ds(0, group - 1)], tok_s)
    all_of(precv, ps)
    all_of(xrecv, xs)
    all_of(acts.at[:, mine, :], as_)
    all_of(rrecv, rs)
    all_of(outg.at[:, pl.ds(0, group - 1)], gs)
    all_of(brecv, bps)


def second_kernel(factor, act_ref, tan_ref, out_ref, buf, sem):
    n, step = buf.shape[:2]
    copies = []
    for j in range(n):
        part = pl.ds(j * step, step)
        buf[j] = factor * lax.dot_general(
            act_ref[:, part], tan_ref[...], (((0,), (0,)), ((), ())), preferred_element_type=F32
        )
        copy = pltpu.make_async_copy(buf.at[j], out_ref.at[part, :], sem.at[j])
        copy.start()
        copies.append(copy)
    for copy in copies:
        copy.wait()


def first_kernel(factor, tok_ref, own_ref, mate_ref, out_ref, both, buf, sem):
    n, step = buf.shape[:2]
    half = own_ref.shape[0]
    both[pl.ds(0, half), :] = own_ref[...]
    both[pl.ds(half, half), :] = mate_ref[...]
    copies = []
    for j in range(n):
        part = pl.ds(j * step, step)
        buf[j] = factor * lax.dot_general(
            tok_ref[:, part], both[...], (((0,), (0,)), ((), ())), preferred_element_type=F32
        )
        copy = pltpu.make_async_copy(buf.at[j], out_ref.at[part, :], sem.at[j])
        copy.start()
        copies.append(copy)
    for copy in copies:
        copy.wait()


def on_device(axes, tokens, first_weight, first_tangent, second_weight, second_tangent):
    tl, dl = tokens.shape
    fl = first_weight.shape[1]
    ncol, ndepth, chips = axes["col"], axes["depth"], axes["row"] // CORES
    group = ncol * ndepth
    total, half = group * tl, group * tl // CORES
    nw, no = pieces(fl, 6), pieces(dl, 3)
    nf = 2 * nw if (fl // nw) % (2 * LANES) == 0 else nw
    cw, ww, dn = fl // nf, fl // nw, dl // no
    far = max(chips - 1, 1)
    groups = GROUPS if nf % GROUPS == 0 else nf
    factor = 1.0 / math.sqrt(total)
    dma = pltpu.SemaphoreType.DMA
    hbm = pl.BlockSpec(memory_space=pl.ANY)
    vmem = pl.BlockSpec(memory_space=pltpu.VMEM)
    gathered, active, out_tan, cross, own_sum, slopes = pl.pallas_call(
        functools.partial(block_kernel, (chips, ncol, ndepth, nw, nf, no)),
        name="block",
        out_shape=(
            jax.ShapeDtypeStruct((total, dl), BF16),
            jax.ShapeDtypeStruct((total, fl), BF16),
            jax.ShapeDtypeStruct((total, dl), BF16),
            jax.ShapeDtypeStruct((half, fl), BF16),
            jax.ShapeDtypeStruct((half, fl), F32),
            jax.ShapeDtypeStruct((half, fl), F32),
        ),
        in_specs=[hbm] * 5,
        out_specs=(vmem,) * 6,
        scratch_shapes=[
            pltpu.VMEM((2, nw, dl, ww), BF16),
            pltpu.VMEM((2, nw, ww, dl), BF16),
            pltpu.VMEM((group, tl, dl), BF16),
            pltpu.VMEM((total, dl), BF16),
            pltpu.VMEM((2, total, fl), F32),
            pltpu.VMEM((nf, 2, half, cw), F32),
            pltpu.VMEM((nf, 2, half, cw), BF16),
            pltpu.VMEM((far, nf, 2, half, cw), BF16),
            pltpu.VMEM((2, total, fl), BF16),
            pltpu.VMEM((no, total, dn), F32),
            pltpu.VMEM((no, group, tl, dn), BF16),
            pltpu.VMEM((no, group - 1, tl, dn), BF16),
            pltpu.VMEM((no, group, tl, dn), BF16),
            pltpu.VMEM((total, fl), F32),
            pltpu.VMEM((groups, half, fl // groups), F32),
            dma((2,)),
            dma,
            dma, dma,
            dma, dma((nf,)),
            dma, dma((far, nf)),
            dma, dma((nf,)),
            dma, dma((no,)),
            dma, dma((no,)),
            dma, dma((groups,)),
        ],
        compiler_params=pltpu.CompilerParams(
            collective_id=0, has_side_effects=True, vmem_limit_bytes=VMEM_MIB * 1024 * 1024
        ),
    )(
        pltpu.with_memory_space_constraint(tokens, pltpu.HBM),
        first_weight, first_tangent, second_weight, second_tangent,
    )

    rows = range(chips * CORES)
    value = own_sum
    arrived = [
        lax.ppermute(cross, "row", [(r, (r + o * CORES) % (chips * CORES)) for r in rows])
        for o in range(1, chips)
    ]
    ns, nd = pieces(fl, STEPS), pieces(dl, STEPS)
    cost = pl.CostEstimate(flops=2 * total * fl * dl, bytes_accessed=4 * fl * dl, transcendentals=0)
    params = pltpu.CompilerParams(vmem_limit_bytes=GRADS_MIB * 1024 * 1024)
    grad_second = pl.pallas_call(
        functools.partial(second_kernel, factor),
        name="second",
        out_shape=jax.ShapeDtypeStruct((fl, dl), F32),
        in_specs=[vmem] * 2,
        out_specs=hbm,
        scratch_shapes=[pltpu.VMEM((ns, fl // ns, dl), F32), dma((ns,))],
        cost_estimate=cost,
        compiler_params=params,
    )(active, out_tan)
    arrived, grad_second = lax.optimization_barrier((arrived, grad_second))
    for part in arrived:
        value = value + part.astype(F32)
    back = (value * slopes).astype(BF16)
    other = lax.ppermute(back, "row", [(r, r + 1 - 2 * (r % CORES)) for r in rows])
    grad_first = pl.pallas_call(
        functools.partial(first_kernel, factor),
        name="first",
        out_shape=jax.ShapeDtypeStruct((dl, fl), F32),
        in_specs=[vmem] * 3,
        out_specs=hbm,
        scratch_shapes=[
            pltpu.VMEM((total, fl), BF16), pltpu.VMEM((nd, dl // nd, fl), F32), dma((nd,))
        ],
        cost_estimate=cost,
        compiler_params=params,
    )(gathered, back, other)
    return grad_first, grad_second


def solution(mesh):
    return jax.shard_map(
        functools.partial(on_device, dict(mesh.shape)),
        mesh=mesh,
        in_specs=(
            P(("col", "depth"), "row"),
            P("row", ("col", "depth")),
            P("row", ("col", "depth")),
            P(("col", "depth"), "row"),
            P(("col", "depth"), "row"),
        ),
        out_specs=(P("row", ("col", "depth")), P(("col", "depth"), "row")),
        check_vma=False,
    )
```

```python
import functools
import math

import jax
import jax.numpy as jnp
from jax import lax
from jax.experimental import pallas as pl
from jax.experimental.pallas import tpu as pltpu
from jax.sharding import PartitionSpec as P

CORES = 2
LAG_CHIP, LAG_SECOND = 3, 2
VMEM_MIB, GRADS_MIB, GROUPS, STEPS = 52, 30, 3, 12
LANES = 128
F32 = jnp.float32
BF16 = jnp.bfloat16


def pieces(extent, most):
    return max(n for n in range(1, most + 1) if extent % (n * LANES) == 0)


def gelu_parts(hidden, hidden_tan):
    inner = 0.7978845608 * (hidden + 0.044715 * hidden * hidden * hidden)
    tval = jnp.tanh(inner)
    active = 0.5 * hidden * (1.0 + tval)
    slopes = 0.5 * (1.0 + tval) + 0.5 * hidden * (1.0 - tval * tval) * 0.7978845608 * (
        1.0 + 3.0 * 0.044715 * hidden * hidden
    )
    return active, slopes * hidden_tan, slopes


def block_kernel(
    sizes,
    tok_ref, fw_ref, ft_ref, sw_ref, st_ref,
    tok_out, act_out, tan2d, cross_out, sum_out, slopes,
    w1, w2, tokg, tok2d, hbuf, precv, xsend, xrecv, acts,
    acc, rsend, rrecv, outg, bbuf, brecv,
    wsem, own_s, tok_s, tok_r,
    ps, pr, xs, xr, as_, ar, rs, rr, gs, gr, bps, bpr,
):
    chips, ncol, ndepth, nw, nf, no = sizes
    group = ncol * ndepth
    tl, dl = tok_ref.shape
    total = group * tl
    half = total // CORES
    ww = w1.shape[-1]
    fl = nw * ww
    cw, dn = fl // nf, dl // no

    row = lax.axis_index("row")
    core = lax.rem(row, CORES)
    chip = lax.div(row, CORES)
    mate = {"row": chip * CORES + (1 - core)}
    across = [{"row": lax.rem(chip + o, chips) * CORES + core} for o in range(1, chips)]
    me = lax.axis_index("col") * ndepth + lax.axis_index("depth")
    ranks = [lax.rem(me + o, group) for o in range(1, group)]
    peers = [{"col": lax.div(r, ndepth), "depth": lax.rem(r, ndepth)} for r in ranks]
    mine = pl.ds(pl.multiple_of(core * half, half), half)
    other = pl.ds(pl.multiple_of((1 - core) * half, half), half)

    barrier = pltpu.get_barrier_semaphore()
    entry = [mate] + across + peers
    for device in entry:
        pl.semaphore_signal(
            barrier, inc=1, device_id=device, device_id_type=pl.DeviceIdType.MESH
        )

    own = pltpu.make_async_copy(tok_ref, tokg.at[me], own_s)
    own.start()
    own.wait()
    loads = {}
    for i, ref in enumerate((fw_ref, ft_ref)):
        for k in range(nw):
            loads[i, k] = pltpu.make_async_copy(
                ref.at[:, pl.ds(k * ww, ww)], w1.at[i, k], wsem.at[0]
            )
    for i, ref in enumerate((sw_ref, st_ref)):
        for k in range(nw):
            loads[2 + i, k] = pltpu.make_async_copy(
                ref.at[pl.ds(k * ww, ww), :], w2.at[i, k], wsem.at[1]
            )
    for pair in (0, 2):
        for k in range(nw):
            loads[pair, k].start()
            loads[pair + 1, k].start()
    def send(src, dst, ssem, rsem, device):
        copy = pltpu.make_async_remote_copy(
            src_ref=src, dst_ref=dst, send_sem=ssem, recv_sem=rsem,
            device_id=device, device_id_type=pl.DeviceIdType.MESH,
        )
        copy.start()
        return copy

    def all_of(ref, sem):
        pltpu.make_async_copy(ref, ref, sem).wait()

    pl.semaphore_wait(barrier, len(entry))

    for device in peers:
        send(tokg.at[me], tokg.at[me], tok_s, tok_r, device)
    all_of(tokg.at[pl.ds(0, group - 1)], tok_r)
    tok2d[...] = tokg[...].astype(F32).reshape(total, dl).astype(BF16)

    tok_out[pl.ds(0, half), :] = tok2d[mine, :]
    tok_out[pl.ds(half, half), :] = tok2d[other, :]

    cols = [pl.ds(k * cw, cw) for k in range(nf)]
    to_mate, to_chips, halves = {}, {}, {}
    per = nf // nw

    all_of(w1, wsem.at[0])

    def first(k):
        for i in range(2):
            weight = w1[i, k // per, :, pl.ds((k % per) * cw, cw)]
            hbuf[i, :, cols[k]] = jnp.dot(tok2d[...], weight, preferred_element_type=F32)
        to_mate[k] = send(hbuf.at[:, other, cols[k]], precv.at[k], ps, pr.at[k], mate)

    def chip_sum(k):
        to_mate[k].wait_recv()
        for i in range(2):
            both = hbuf[i, mine, cols[k]] + precv[k, i]
            hbuf[i, mine, cols[k]] = both
            xsend[k, i] = both.astype(BF16)
        to_chips[k] = [
            send(xsend.at[k], xrecv.at[o, k], xs, xr.at[o, k], device)
            for o, device in enumerate(across)
        ]

    def activate(k):
        hidden, hidden_tan = hbuf[0, mine, cols[k]], hbuf[1, mine, cols[k]]
        for o, copy in enumerate(to_chips[k]):
            copy.wait_recv()
            hidden = hidden + xrecv[o, k, 0].astype(F32)
            hidden_tan = hidden_tan + xrecv[o, k, 1].astype(F32)
        active, active_tan, slope = gelu_parts(hidden, hidden_tan)
        acts[0, mine, cols[k]] = active_tan.astype(BF16)
        acts[1, mine, cols[k]] = active.astype(BF16)
        slopes[:, cols[k]] = slope
        part = acts.at[:, mine, cols[k]]
        halves[k] = send(part, part, as_, ar.at[k], mate)

    def second(k, begin, last):
        for j in range(begin, k + 1):
            halves[j].wait_recv()
        w, base = begin // per, (begin % per) * cw
        span, here = (k + 1 - begin) * cw, pl.ds(begin * cw, (k + 1 - begin) * cw)
        if begin == 0:
            all_of(w2, wsem.at[1])
        for n in range(no):
            part = pl.ds(n * dn, dn)
            term = None
            for i in range(2):
                product = jnp.dot(
                    acts[i, :, here], w2[i, w, pl.ds(base, span), part], preferred_element_type=F32
                )
                term = product if term is None else term + product
            if begin > 0:
                term += acc[n]
            acc[n] = term
            if last:
                rsend[n] = term.reshape(group, tl, dn).astype(BF16)
                for o, (r, device) in enumerate(zip(ranks, peers)):
                    send(rsend.at[n, r], rrecv.at[n, o], rs, rr.at[n], device)

    for t in range(nf + LAG_CHIP):
        if t < nf:
            first(t)
        if t >= LAG_CHIP:
            chip_sum(t - LAG_CHIP)
    begin = 0
    for t in range(nf + LAG_SECOND):
        if t < nf:
            activate(t)
        k = t - LAG_SECOND
        if k >= 0 and ((k + 1) % per == 0 or k // per == nw - 1):
            second(k, begin, k == nf - 1)
            begin = k + 1
    act_out[...] = acts[1]

    for n in range(no):
        value = acc[n, pl.ds(pl.multiple_of(me * tl, tl), tl), :]
        all_of(rrecv.at[n], rr.at[n])
        for o in range(group - 1):
            value += rrecv[n, o].astype(F32)
        outg[n, me] = value.astype(BF16)
        for device in peers:
            send(outg.at[n, me], outg.at[n, me], gs, gr.at[n], device)

    to_mate = {}
    wide = nf // GROUPS if nf % GROUPS == 0 else 1

    def back_chip_sum(g):
        to_mate[g].wait_recv()
        span = pl.ds(g * wide * cw, wide * cw)
        both = bbuf[mine, span] + brecv[g]
        sum_out[:, span] = both
        cross_out[:, span] = both.astype(BF16)

    for n in range(no):
        all_of(outg.at[n, pl.ds(0, group - 1)], gr.at[n])
        part = pl.ds(n * dn, dn)
        tan2d[:, part] = outg[n].astype(F32).reshape(total, dn).astype(BF16)
        for k in range(nf):
            term = lax.dot_general(
                tan2d[:, part], w2[0, k // per, pl.ds((k % per) * cw, cw), part],
                (((1,), (1,)), ((), ())), preferred_element_type=F32,
            )
            if n > 0:
                term += bbuf[:, cols[k]]
            bbuf[:, cols[k]] = term
            if n == no - 1 and (k + 1) % wide == 0:
                g = k // wide
                span = pl.ds(g * wide * cw, wide * cw)
                to_mate[g] = send(bbuf.at[other, span], brecv.at[g], bps, bpr.at[g], mate)
    for g in range(nf // wide):
        back_chip_sum(g)
    all_of(tokg.at[pl.ds(0, group - 1)], tok_s)
    all_of(precv, ps)
    all_of(xrecv, xs)
    all_of(acts.at[:, mine, :], as_)
    all_of(rrecv, rs)
    all_of(outg.at[:, pl.ds(0, group - 1)], gs)
    all_of(brecv, bps)


def second_kernel(factor, act_ref, tan_ref, out_ref, buf, sem):
    n, step = buf.shape[:2]
    copies = []
    for j in range(n):
        part = pl.ds(j * step, step)
        buf[j] = factor * lax.dot_general(
            act_ref[:, part], tan_ref[...], (((0,), (0,)), ((), ())), preferred_element_type=F32
        )
        copy = pltpu.make_async_copy(buf.at[j], out_ref.at[part, :], sem.at[j])
        copy.start()
        copies.append(copy)
    for copy in copies:
        copy.wait()


def first_kernel(factor, tok_ref, own_ref, mate_ref, out_ref, both, buf, sem):
    n, step = buf.shape[:2]
    half = own_ref.shape[0]
    both[pl.ds(0, half), :] = own_ref[...]
    both[pl.ds(half, half), :] = mate_ref[...]
    copies = []
    for j in range(n):
        part = pl.ds(j * step, step)
        buf[j] = factor * lax.dot_general(
            tok_ref[:, part], both[...], (((0,), (0,)), ((), ())), preferred_element_type=F32
        )
        copy = pltpu.make_async_copy(buf.at[j], out_ref.at[part, :], sem.at[j])
        copy.start()
        copies.append(copy)
    for copy in copies:
        copy.wait()


def on_device(axes, tokens, first_weight, first_tangent, second_weight, second_tangent):
    tl, dl = tokens.shape
    fl = first_weight.shape[1]
    ncol, ndepth, chips = axes["col"], axes["depth"], axes["row"] // CORES
    group = ncol * ndepth
    total, half = group * tl, group * tl // CORES
    nw, no = pieces(fl, 6), pieces(dl, 3)
    nf = 2 * nw if (fl // nw) % (2 * LANES) == 0 else nw
    cw, ww, dn = fl // nf, fl // nw, dl // no
    far = max(chips - 1, 1)
    groups = GROUPS if nf % GROUPS == 0 else nf
    factor = 1.0 / math.sqrt(total)
    dma = pltpu.SemaphoreType.DMA
    hbm = pl.BlockSpec(memory_space=pl.ANY)
    vmem = pl.BlockSpec(memory_space=pltpu.VMEM)
    gathered, active, out_tan, cross, own_sum, slopes = pl.pallas_call(
        functools.partial(block_kernel, (chips, ncol, ndepth, nw, nf, no)),
        name="block",
        out_shape=(
            jax.ShapeDtypeStruct((total, dl), BF16),
            jax.ShapeDtypeStruct((total, fl), BF16),
            jax.ShapeDtypeStruct((total, dl), BF16),
            jax.ShapeDtypeStruct((half, fl), BF16),
            jax.ShapeDtypeStruct((half, fl), F32),
            jax.ShapeDtypeStruct((half, fl), F32),
        ),
        in_specs=[hbm] * 5,
        out_specs=(vmem,) * 6,
        scratch_shapes=[
            pltpu.VMEM((2, nw, dl, ww), BF16),
            pltpu.VMEM((2, nw, ww, dl), BF16),
            pltpu.VMEM((group, tl, dl), BF16),
            pltpu.VMEM((total, dl), BF16),
            pltpu.VMEM((2, total, fl), F32),
            pltpu.VMEM((nf, 2, half, cw), F32),
            pltpu.VMEM((nf, 2, half, cw), BF16),
            pltpu.VMEM((far, nf, 2, half, cw), BF16),
            pltpu.VMEM((2, total, fl), BF16),
            pltpu.VMEM((no, total, dn), F32),
            pltpu.VMEM((no, group, tl, dn), BF16),
            pltpu.VMEM((no, group - 1, tl, dn), BF16),
            pltpu.VMEM((no, group, tl, dn), BF16),
            pltpu.VMEM((total, fl), F32),
            pltpu.VMEM((groups, half, fl // groups), F32),
            dma((2,)),
            dma,
            dma, dma,
            dma, dma((nf,)),
            dma, dma((far, nf)),
            dma, dma((nf,)),
            dma, dma((no,)),
            dma, dma((no,)),
            dma, dma((groups,)),
        ],
        compiler_params=pltpu.CompilerParams(
            collective_id=0, has_side_effects=True, vmem_limit_bytes=VMEM_MIB * 1024 * 1024
        ),
    )(
        pltpu.with_memory_space_constraint(tokens, pltpu.HBM),
        first_weight, first_tangent, second_weight, second_tangent,
    )

    rows = range(chips * CORES)
    value = own_sum
    arrived = [
        lax.ppermute(cross, "row", [(r, (r + o * CORES) % (chips * CORES)) for r in rows])
        for o in range(1, chips)
    ]
    ns, nd = pieces(fl, STEPS), pieces(dl, STEPS)
    cost = pl.CostEstimate(flops=2 * total * fl * dl, bytes_accessed=4 * fl * dl, transcendentals=0)
    params = pltpu.CompilerParams(vmem_limit_bytes=GRADS_MIB * 1024 * 1024)
    grad_second = pl.pallas_call(
        functools.partial(second_kernel, factor),
        name="second",
        out_shape=jax.ShapeDtypeStruct((fl, dl), F32),
        in_specs=[vmem] * 2,
        out_specs=hbm,
        scratch_shapes=[pltpu.VMEM((ns, fl // ns, dl), F32), dma((ns,))],
        cost_estimate=cost,
        compiler_params=params,
    )(active, out_tan)
    arrived, grad_second = lax.optimization_barrier((arrived, grad_second))
    for part in arrived:
        value = value + part.astype(F32)
    back = (value * slopes).astype(BF16)
    other = lax.ppermute(back, "row", [(r, r + 1 - 2 * (r % CORES)) for r in rows])
    grad_first = pl.pallas_call(
        functools.partial(first_kernel, factor),
        name="first",
        out_shape=jax.ShapeDtypeStruct((dl, fl), F32),
        in_specs=[vmem] * 3,
        out_specs=hbm,
        scratch_shapes=[
            pltpu.VMEM((total, fl), BF16), pltpu.VMEM((nd, dl // nd, fl), F32), dma((nd,))
        ],
        cost_estimate=cost,
        compiler_params=params,
    )(gathered, back, other)
    return grad_first, grad_second


def solution(mesh):
    return jax.shard_map(
        functools.partial(on_device, dict(mesh.shape)),
        mesh=mesh,
        in_specs=(
            P(("col", "depth"), "row"),
            P("row", ("col", "depth")),
            P("row", ("col", "depth")),
            P(("col", "depth"), "row"),
            P(("col", "depth"), "row"),
        ),
        out_specs=(P("row", ("col", "depth")), P(("col", "depth"), "row")),
        check_vma=False,
    )
```
